32 devices in a mesh: groups: 2 (over y), deg: 4 (over z), sub: 2 (over x), fld: 2 (over core).
Axes of the slice: x: 2, y: 2, z: 4, core: 2. Of those that a mesh axis runs over, the one named last changes fastest.
Arguments:
- coefficients: bfloat16 [32, 2, 32, 2048], P(None, None, ('groups', 'fld'), ('deg', 'sub')), parts along dimension 2, may hold values from -6 to 6
- delta: bfloat16 [32, 2, 2048, 2048], P('deg', None, None, 'sub'), may hold values from -0.125 to 0.125
- order_of: int32 [2048], replicated, may hold values from 0 to 2047, each once
- degree_of: int32 [32], replicated, may hold values from 512 to 2047
- angle_index: int32 [32, 3], P(('groups', 'fld')), parts along dimension 0, may hold values from 0 to 4095
Outputs:
- rotated: float32 [32, 2, 32, 2048], P(None, None, ('groups', 'fld'), ('deg', 'sub')), parts along dimension 2
The draws below stay inside these ranges and needn't reach their ends.
There are 2 independent parts, one for each index of `groups`. The reference program is written for one: setup_inputs(seed, part) draws one part's arguments, and reference() takes and returns one part's arrays. A program takes and returns all parts, laid end to end along the dimension named above; an argument that names none is the same for every part. Nothing has to cross between parts.
All inputs are finite; a program needn't handle non-finite values.
Results may differ from the reference program's by a relative error of at most 0.004.
Values may be sent and summed in bfloat16 or wider, within the bound.
No kernel may reach another device: no remote copies, remote signals or barrier semaphores. Data moves between devices by JAX's collectives and lax.ppermute only.
A program may use at most 128 MiB of HBM per device.

```python
import math
import jax
import jax.numpy as jnp
from jax import lax

NM = 2048
FIELDS = 16
NANG = 4096
NDEG = 32


def touch_ends(entries, own_key, low, high):
    dims = entries.shape
    spot = [jax.random.randint(jax.random.fold_in(own_key, axis), (), 0, dims[axis]) for axis in range(len(dims))]
    entries = entries.at[tuple(spot)].set(low)
    longest = dims.index(max(dims))
    spot[longest] = (spot[longest] + 1) % dims[longest]
    return entries.at[tuple(spot)].set(high)


def steps_of(key, shape, cuts, low, high):
    def one(position, parts):
        draws = jax.random.uniform(jax.random.fold_in(jax.random.fold_in(key, 6), position), (parts,), jnp.float32, low / len(cuts), high / len(cuts))
        return jnp.repeat(jnp.exp(draws), shape[position] // parts).reshape((-1,) + (1,) * (len(shape) - position - 1))

    level = one(*cuts[0])
    for cut in cuts[1:]:
        level = level * one(*cut)
    return level


def bell_draw(rng, dims, width, limit, shards=(), held_as=jnp.bfloat16):
    values = jax.random.normal(rng, dims, jnp.float32) * width
    if len(shards) > 0:
        values = steps_of(rng, dims, shards, -0.22, 0.18) * values
    return jnp.clip(values, min=-limit, max=limit).astype(held_as)


def setup_inputs(seed: int = 0, part: int = 0) -> dict:
    key_of = jax.random.split(jax.random.key(seed), 6)
    part_keys = jax.random.split(jax.random.fold_in(key_of[5], part), 6)
    return {
        "coefficients": bell_draw(part_keys[0], (NDEG, 2, FIELDS, NM), 1.0, 6.0, ((2, 2), (3, 8))),
        "delta": bell_draw(key_of[1], (NDEG, 2, NM, NM), NM ** -0.5, 0.125, ((0, 4), (3, 2))),
        "order_of": jax.random.permutation(key_of[2], NM).astype(jnp.int32),
        "degree_of": touch_ends(jax.random.randint(key_of[3], (NDEG,), NM // 4, NM), jax.random.fold_in(key_of[3], 1), NM // 4, NM - 1).astype(jnp.int32),
        "angle_index": touch_ends(jax.random.randint(part_keys[4], (FIELDS, 3), 0, NANG), jax.random.fold_in(part_keys[4], 1), 0, NANG - 1).astype(jnp.int32),
    }


def phase_pair(angle_index, column, orders):
    steps_int = (angle_index[:, column][:, None] * orders[None, :]) % NANG
    angle_val = steps_int.astype(jnp.float32) * (2.0 * math.pi / NANG)
    return jnp.cos(angle_val), jnp.sin(angle_val)


def twist_phase(values, cosine, sine):
    cos_part = values[:, 0]
    sin_part = values[:, 1]
    return jnp.stack([cosine * cos_part - sine * sin_part, sine * cos_part + cosine * sin_part], axis=1)


def live_mask(degrees, orders):
    limits = degrees[:, None]
    cosine_live = orders[None, :] <= limits
    sine_live = cosine_live & (orders[None, :] >= 1)
    return jnp.stack([cosine_live, sine_live], axis=1)[:, :, None, :].astype(jnp.float32)


def reference(coefficients, delta, order_of, degree_of, angle_index):
    natural = jnp.zeros_like(coefficients).at[:, :, :, order_of].set(coefficients)
    orders = jnp.arange(NM, dtype=jnp.int32)
    alpha_cos, alpha_sin = phase_pair(angle_index, 0, orders)
    beta_cos, beta_sin = phase_pair(angle_index, 1, orders)
    gamma_cos, gamma_sin = phase_pair(angle_index, 2, orders)

    def one_degree(packed):
        values, table, degree = packed
        live = live_mask(degree[None], orders)
        table_f = table.astype(jnp.float32)
        first_turn = twist_phase(live * values[None].astype(jnp.float32), gamma_cos, gamma_sin).astype(jnp.bfloat16)
        turned = live * jnp.einsum("kpfm,pmn->kpfn", first_turn.astype(jnp.float32), table_f)
        middle = twist_phase(turned, beta_cos, beta_sin).astype(jnp.bfloat16)
        second = live * jnp.einsum("kpfm,pmn->kpfn", middle.astype(jnp.float32), table_f)
        return twist_phase(second, alpha_cos, alpha_sin)[0]

    result = lax.map(one_degree, (natural, delta, degree_of))
    return jnp.take(result, order_of, axis=3)
```

```python
import functools
import math

import jax
import jax.numpy as jnp
from jax import lax
from jax.experimental import pallas as pl
from jax.experimental.pallas import tpu as pltpu
from jax.sharding import PartitionSpec as P

NANG = 4096
F32 = jnp.float32
BF16 = jnp.bfloat16
VMEM = pl.BlockSpec(memory_space=pltpu.VMEM)
SMEM = pl.BlockSpec(memory_space=pltpu.SMEM)
ANY = pl.BlockSpec(memory_space=pl.ANY)
MIB = 1 << 20


def phases(angles, orders):
    steps = (angles * orders) & (NANG - 1)
    turn = steps.astype(F32) * (2.0 * math.pi / NANG)
    return jnp.cos(turn), jnp.sin(turn)


def live_pair(orders, degree):
    cosine = (orders <= degree).astype(F32)
    return cosine, jnp.where(orders >= 1, cosine, 0.0)


def call(kernel, outs, ins, in_specs, out_specs, name, flops=0, moved=0, scratch=(), vmem=8 * MIB):
    return pl.pallas_call(
        kernel,
        out_shape=outs,
        in_specs=in_specs,
        out_specs=out_specs,
        scratch_shapes=list(scratch),
        name=name,
        cost_estimate=pl.CostEstimate(flops=flops, bytes_accessed=moved, transcendentals=0),
        compiler_params=pltpu.CompilerParams(vmem_limit_bytes=vmem),
    )(*ins)


def first_kernel(sizes, meta, degree, coef, order, angle, *outs):
    n_deg, n_fld, n_own, n_f = sizes
    me_fld = meta[2]
    orders = order[...]
    cosine, sine = phases(angle[:, 2:3], orders)

    @pl.loop(0, n_deg)
    def _(d):
        for j in range(n_fld):
            for k in range(n_own):
                slot = d * (n_fld * n_own) + (me_fld ^ j) * n_own + k
                live_c, live_s = live_pair(orders, degree[slot])
                c = live_c * coef[slot, 0].astype(F32)
                s = live_s * coef[slot, 1].astype(F32)
                both = jnp.concatenate([cosine * c - sine * s, sine * c + cosine * s], axis=0)
                outs[j][d, k * 2 * n_f : (k + 1) * 2 * n_f, :] = both.astype(BF16)


def select_kernel(cols, meta, order, angle, p_ref, q_ref, cos_ref, sin_ref):
    n_m = order.shape[1]
    base = meta[1] * cols
    orders = order[...]
    step = 128
    for b in range(n_m // step):
        row = orders[:, b * step : (b + 1) * step]
        column = jnp.broadcast_to(row, (step, step)).T
        for m in range(n_m // step):
            lanes = lax.broadcasted_iota(jnp.int32, (step, step), 1) + m * step
            p_ref[b * step : (b + 1) * step, m * step : (m + 1) * step] = jnp.where(column == lanes, 1.0, 0.0).astype(BF16)
    rows = min(cols, 128)

    @pl.loop(0, cols // rows)
    def _(b):
        first = pl.multiple_of(b * rows, rows)
        index = lax.broadcasted_iota(jnp.int32, (rows, n_m), 0) + (base + first)
        q_ref[pl.ds(first, rows), :] = jnp.where(index == orders, 1.0, 0.0).astype(BF16)

    columns = lax.broadcasted_iota(jnp.int32, (1, cols), 1) + base
    cosine, sine = phases(angle[:, 1:2], columns)
    cos_ref[...] = cosine
    sin_ref[...] = sine


def fetch_kernel(n_own, k, meta, table, out, sem):
    copy = pltpu.make_async_copy(table.at[meta[2] * n_own + k], out, sem)
    copy.start()
    copy.wait()


def spread(pieces, p_ref, first):
    n_m = p_ref.shape[1]
    block = min(n_m, 1024)
    out = []
    for b in range(n_m // block):
        at, total = first, None
        for piece in pieces:
            width = piece.shape[1]
            part = jnp.dot(
                piece[...], p_ref[at : at + width, b * block : (b + 1) * block], preferred_element_type=F32
            )
            total = part if total is None else total + part
            at += width
        out.append(total)
    return out


def spread_kernel(n, *refs):
    pieces, (p_ref, out) = refs[:n], refs[n:]
    parts = spread(pieces, p_ref, 0)
    block = parts[0].shape[1]
    for b, part in enumerate(parts):
        out[:, b * block : (b + 1) * block] = part.astype(BF16)


def turn_kernel(n, sizes, meta, degree, *refs):
    n_deg, n_fld, n_own, n_f, cols = sizes
    pieces = refs[:n]
    half, p_ref, cos_ref, sin_ref = refs[n : n + 4]
    tables = refs[n + 4 : n + 4 + n_own]
    out, natural = refs[n + 4 + n_own :]
    first = p_ref.shape[0] - sum(piece.shape[1] for piece in pieces)
    parts = spread(pieces, p_ref, first)
    block = parts[0].shape[1]
    per = 2 * n_own * n_f
    for b, part in enumerate(parts):
        part = part + half[:, b * block : (b + 1) * block].astype(F32)
        for r in range(2 * n_own):
            rows = [part[j * per + r * n_f : j * per + (r + 1) * n_f] for j in range(n_fld)]
            natural[r, :, b * block : (b + 1) * block] = jnp.concatenate(rows, axis=0).astype(BF16)
    columns = lax.broadcasted_iota(jnp.int32, (1, cols), 1) + meta[1] * cols
    own = meta[0] * (n_fld * n_own) + meta[2] * n_own
    for k in range(n_own):
        live_c, live_s = live_pair(columns, degree[own + k])
        c = live_c * jnp.dot(natural[2 * k], tables[k][0], preferred_element_type=F32)
        s = live_s * jnp.dot(natural[2 * k + 1], tables[k][1], preferred_element_type=F32)
        cosine, sine = cos_ref[...], sin_ref[...]
        out[2 * k] = (cosine * c - sine * s).astype(BF16)
        out[2 * k + 1] = (sine * c + cosine * s).astype(BF16)


def part_kernel(n_own, cols, meta, mid, *refs):
    tables, out = refs[:n_own], refs[n_own]
    at = pl.multiple_of(meta[1] * cols, cols)
    for k in range(n_own):
        for p in range(2):
            out[2 * k + p] = jnp.dot(mid[2 * k + p], tables[k][p, pl.ds(at, cols), :], preferred_element_type=F32)


def second_kernel(n, sizes, meta, degree, *refs):
    n_deg, n_fld, n_own, n_f, cols = sizes
    mids = refs[:n]
    part, q_ref = refs[n : n + 2]
    tables = refs[n + 2 : n + 2 + n_own]
    outs, held = refs[n + 2 + n_own : -1], refs[-1]
    columns = lax.broadcasted_iota(jnp.int32, (1, cols), 1) + meta[1] * cols
    own = meta[0] * (n_fld * n_own) + meta[2] * n_own
    per = 2 * n_own * n_f
    for k in range(n_own):
        lives = live_pair(columns, degree[own + k])
        both = []
        for p in range(2):
            r = 2 * k + p
            total = part[r]
            for i, mid in enumerate(mids):
                at = pl.multiple_of((meta[1] ^ (i + 1)) * cols, cols)
                total += jnp.dot(mid[r], tables[k][p, pl.ds(at, cols), :], preferred_element_type=F32)
            both.append(lives[p] * total)
        for j in range(n_fld):
            rows = jnp.concatenate([x[j * n_f : (j + 1) * n_f] for x in both], axis=0)
            at = j * per + 2 * k * n_f
            held[at : at + 2 * n_f, :] = rows.astype(BF16)
    at = 0
    for out in outs:
        width = out.shape[1]
        out[...] = jnp.dot(held[...], q_ref[:, at : at + width], preferred_element_type=F32).astype(BF16)
        at += width


def last_kernel(sizes, meta, order, angle, own, got, out):
    n_deg, n_fld, n_own, n_f = sizes
    cosine, sine = phases(angle[:, 0:1], order[...])
    for j, ref in enumerate((own, got)):
        for d in range(n_deg):
            at = (meta[0] ^ d) * (n_fld * n_own) + (meta[2] ^ j) * n_own
            for k in range(n_own):
                rows = ref[d, 2 * k * n_f : 2 * (k + 1) * n_f, :].astype(F32)
                c, s = rows[:n_f], rows[n_f:]
                out[at + k, 0] = cosine * c - sine * s
                out[at + k, 1] = sine * c + cosine * s


def xor_pairs(size, x):
    return [(i, i ^ x) for i in range(size)]


def per_device(coefficients, delta, order_of, degree_of, angle_index):
    n_deg, n_sub, n_fld = (lax.axis_size(a) for a in ("deg", "sub", "fld"))
    held_deg, _, n_m, cols = delta.shape
    n_f, slots = coefficients.shape[2:]
    n_own = held_deg // n_fld
    sizes = (n_deg, n_fld, n_own, n_f)
    rows = n_fld * 2 * n_own * n_f
    d, s, c = (lax.axis_index(a) for a in ("deg", "sub", "fld"))
    meta = jnp.stack([d, s, c]).astype(jnp.int32)
    shape = jax.ShapeDtypeStruct

    def swap(x, axis, k):
        return lax.ppermute(x, axis, xor_pairs(lax.axis_size(axis), k))

    order_table = order_of.reshape(n_deg, n_sub, slots)
    my_order = lax.dynamic_slice_in_dim(order_of, (d * n_sub + s) * slots, slots).reshape(1, slots)
    relative = order_table[(d ^ jnp.arange(n_deg))[None, :], (s ^ jnp.arange(n_sub))[:, None]].reshape(1, n_m)
    angles = jnp.concatenate([angle_index] + [swap(angle_index, "fld", j) for j in range(1, n_fld)], axis=0)

    firsts = call(
        functools.partial(first_kernel, sizes),
        [shape((n_deg, 2 * n_own * n_f, slots), BF16)] * n_fld,
        (meta, degree_of, coefficients, my_order, angle_index),
        [SMEM, SMEM, VMEM, VMEM, VMEM],
        [VMEM] * n_fld,
        "first",
        moved=2 * coefficients.size * 2,
    )
    firsts = [firsts[0]] + [swap(firsts[j], "fld", j) for j in range(1, n_fld)]

    p_ref, q_ref, cos_ref, sin_ref = call(
        functools.partial(select_kernel, cols),
        [pltpu.VMEM((n_m, n_m), BF16), pltpu.VMEM((cols, n_m), BF16)] + [pltpu.VMEM((n_fld * n_f, cols), F32)] * 2,
        (meta, relative, angles),
        [SMEM, VMEM, VMEM],
        [VMEM] * 4,
        "select",
        moved=2 * n_m * (n_m + cols),
    )
    tables = [
        call(
            functools.partial(fetch_kernel, n_own, k),
            pltpu.VMEM((2, n_m, cols), BF16),
            (meta, delta),
            [SMEM, ANY],
            VMEM,
            f"fetch{k}",
            moved=4 * n_m * cols,
            scratch=[pltpu.SemaphoreType.DMA],
        )
        for k in range(n_own)
    ]

    def block(j):
        return jnp.concatenate([lax.dynamic_index_in_dim(x, d ^ j, 0, keepdims=False) for x in firsts], axis=0)

    arrived = [block(0)] + [swap(block(j), "deg", j) for j in range(1, n_deg)]
    mine = jnp.concatenate(arrived, axis=1)
    others = [swap(mine, "sub", i) for i in range(1, n_sub)]
    half = call(
        functools.partial(spread_kernel, 1),
        pltpu.VMEM((rows, n_m), BF16),
        (mine, p_ref),
        [VMEM] * 2,
        VMEM,
        "spread",
        flops=2 * rows * n_deg * slots * n_m,
    )
    n = len(others)
    mid = call(
        functools.partial(turn_kernel, n, sizes + (cols,)),
        shape((2 * n_own, n_fld * n_f, cols), BF16),
        (meta, degree_of, *others, half, p_ref, cos_ref, sin_ref, *tables),
        [SMEM] * 2 + [VMEM] * (n + 4 + n_own),
        VMEM,
        "turn",
        flops=2 * rows * n_m * (n_m + cols),
        scratch=[pltpu.VMEM((2 * n_own, n_fld * n_f, n_m), BF16)],
    )
    mids = [swap(mid, "sub", i) for i in range(1, n_sub)]
    part = call(
        functools.partial(part_kernel, n_own, cols),
        pltpu.VMEM((2 * n_own, n_fld * n_f, cols), F32),
        (meta, mid, *tables),
        [SMEM] + [VMEM] * (1 + n_own),
        VMEM,
        "part",
        flops=2 * rows * cols * cols,
    )
    outs = call(
        functools.partial(second_kernel, n, sizes + (cols,)),
        [shape((rows, n_deg * slots), BF16)] * n_sub,
        (meta, degree_of, *mids, part, q_ref, *tables),
        [SMEM] * 2 + [VMEM] * (n + 2 + n_own),
        [VMEM] * n_sub,
        "second",
        flops=2 * rows * cols * (n_m - cols + n_m),
        scratch=[pltpu.VMEM((rows, cols), BF16)],
    )
    total = outs[0]
    for i in range(1, n_sub):
        total = total + swap(outs[i], "sub", i)
    blocks = [total[:, j * slots : (j + 1) * slots] for j in range(n_deg)]
    blocks = [blocks[0]] + [swap(blocks[j], "deg", j) for j in range(1, n_deg)]
    stacked = jnp.stack(blocks)
    per = 2 * n_own * n_f
    parts = [stacked[:, j * per : (j + 1) * per] for j in range(n_fld)]
    parts = [parts[0]] + [swap(parts[j], "fld", j) for j in range(1, n_fld)]
    return call(
        functools.partial(last_kernel, sizes),
        shape((n_deg * held_deg,) + coefficients.shape[1:], F32),
        (meta, my_order, angle_index, *parts),
        [SMEM] + [VMEM] * (2 + n_fld),
        VMEM,
        "last",
        moved=6 * coefficients.size,
    )


def solution(mesh):
    in_specs = (
        P(None, None, ("groups", "fld"), ("deg", "sub")),
        P("deg", None, None, "sub"),
        P(),
        P(),
        P(("groups", "fld"), None),
    )
    out_specs = P(None, None, ("groups", "fld"), ("deg", "sub"))
    return jax.shard_map(per_device, mesh=mesh, in_specs=in_specs, out_specs=out_specs, check_vma=False)
```

```python
import functools
import math

import jax
import jax.numpy as jnp
from jax import lax
from jax.experimental import pallas as pl
from jax.experimental.pallas import tpu as pltpu
from jax.sharding import PartitionSpec as P

NANG = 4096
CODE = 64
LANES = 128
F32 = jnp.float32
BF16 = jnp.bfloat16
VMEM = pl.BlockSpec(memory_space=pltpu.VMEM)
SMEM = pl.BlockSpec(memory_space=pltpu.SMEM)
HBM = pl.BlockSpec(memory_space=pltpu.HBM)
MIB = 1 << 20


class Sizes:
    def __init__(self, coefficients, delta):
        self.deg, self.sub, self.fld = (lax.axis_size(a) for a in ("deg", "sub", "fld"))
        self.held, _, self.orders, self.cols = delta.shape
        self.fields, self.slots = coefficients.shape[2:]
        self.own = self.held // self.fld
        self.per = 2 * self.own * self.fields
        self.rows = self.fld * self.per
        self.chunks = 2 if self.own % 2 == 0 else 1
        self.kept = self.own // self.chunks
        self.whole_rows = self.slots % LANES == 0


def here():
    return lax.axis_index("deg"), lax.axis_index("sub"), lax.axis_index("fld")


def phases(angles, orders):
    steps = (angles * orders) & (NANG - 1)
    turn = steps.astype(F32) * (2.0 * math.pi / NANG)
    return jnp.cos(turn), jnp.sin(turn)


def column(ref, which, count):
    rows = lax.broadcasted_iota(jnp.int32, (count, 1), 0)
    out = jnp.zeros((count, 1), jnp.int32)
    for f in range(count):
        out = jnp.where(rows == f, ref[which, f], out)
    return out


def own_orders(z, order):
    if not z.whole_rows:
        return order[...]
    d, s, _ = here()
    n = z.slots // LANES
    rows = [order[pl.ds((d * z.sub + s) * n + b, 1), :] for b in range(n)]
    return jnp.concatenate(rows, axis=1)


def relative_orders(z, order):
    if not z.whole_rows:
        return [order[b : b + 1, :] for b in range(z.orders // LANES)]
    d, s, _ = here()
    n = z.slots // LANES
    return [
        order[pl.ds(((d ^ j) * z.sub + (s ^ i)) * n + b, 1), :]
        for i in range(z.sub)
        for j in range(z.deg)
        for b in range(n)
    ]


def live_pair(orders, degree):
    cosine = (orders <= degree).astype(F32)
    return cosine, jnp.where(orders >= 1, cosine, 0.0)


def pinned(x):
    return pltpu.with_memory_space_constraint(x, pltpu.HBM)


def call(kernel, outs, ins, in_specs, out_specs, name, flops=0, moved=0, scratch=(), vmem=4 * MIB):
    ins = [pinned(x) if spec is HBM else x for x, spec in zip(ins, in_specs)]
    return pl.pallas_call(
        kernel,
        out_shape=outs,
        in_specs=in_specs,
        out_specs=out_specs,
        scratch_shapes=list(scratch),
        name=name,
        cost_estimate=pl.CostEstimate(flops=flops, bytes_accessed=moved, transcendentals=0),
        compiler_params=pltpu.CompilerParams(vmem_limit_bytes=vmem),
    )(*ins)


def first_kernel(z, coef_hbm, degree_hbm, order_hbm, angle_hbm, *refs):
    outs, (coef, degree, order, angle, sems) = refs[: z.fld], refs[z.fld :]
    copies = [
        pltpu.make_async_copy(a, b, sems.at[i])
        for i, (a, b) in enumerate(
            ((order_hbm, order), (angle_hbm, angle), (degree_hbm, degree), (coef_hbm, coef))
        )
    ]
    for copy in copies:
        copy.start()
    for copy in copies[:2]:
        copy.wait()
    d, _, c = here()
    orders = own_orders(z, order)
    angles = column(angle, 2, z.fields)
    cosine, sine = phases(angles, orders)
    for copy in copies[2:]:
        copy.wait()
    for j in range(1, z.fld):
        beta = jnp.broadcast_to(column(angle, 1, z.fields), (z.fields, z.slots))
        code = jnp.concatenate([beta // CODE, beta % CODE], axis=0)
        outs[j][z.deg * z.per :, :] = code.astype(F32).astype(BF16)

    def one(b):
        for j in range(z.fld):
            for k in range(z.own):
                slot = (d ^ b) * z.held + (c ^ j) * z.own + k
                live_c, live_s = live_pair(orders, degree[slot])
                x = live_c * coef[slot, 0].astype(F32)
                y = live_s * coef[slot, 1].astype(F32)
                both = jnp.concatenate([cosine * x - sine * y, sine * x + cosine * y], axis=0)
                at = b * z.per + k * 2 * z.fields
                if not isinstance(b, int):
                    at = pl.multiple_of(at, 2 * z.fields)
                outs[j][pl.ds(at, 2 * z.fields), :] = both.astype(BF16)

    if z.deg <= 4:
        for b in range(z.deg):
            one(b)
    else:
        pl.loop(0, z.deg)(one)


def fetches(z, table, picks, outs, sems):
    first = lax.axis_index("fld") * z.own
    copies = []
    for n, (pick, out) in enumerate(zip(picks, outs)):
        pieces = sems.shape[1]
        step = z.orders // pieces
        copies.append(
            [
                pltpu.make_async_copy(
                    table.at[first + pick // 2, pick % 2, pl.ds(i * step, step)],
                    out.at[pl.ds(i * step, step)],
                    sems.at[n, i],
                )
                for i in range(pieces)
            ]
        )
    for group in copies:
        for copy in group:
            copy.start()
    return copies


def finish(copies):
    for group in copies:
        for copy in group:
            copy.wait()


def select_kernel(z, picks, order, angle_hbm, table, *refs):
    got, refs = refs[: z.fld - 1], refs[z.fld - 1 :]
    p_ref, cos_ref, sin_ref = refs[:3]
    outs, (angle, sem, sems) = refs[3 : 3 + len(picks)], refs[3 + len(picks) :]
    copies = fetches(z, table, picks, outs, sems)
    copy = pltpu.make_async_copy(angle_hbm, angle, sem)
    copy.start()
    base = lax.axis_index("sub") * z.cols
    for b, row in enumerate(relative_orders(z, order)):
        slots = jnp.broadcast_to(row, (LANES, LANES)).T
        for m in range(z.orders // LANES):
            lanes = lax.broadcasted_iota(jnp.int32, (LANES, LANES), 1) + m * LANES
            p_ref[b * LANES : (b + 1) * LANES, m * LANES : (m + 1) * LANES] = jnp.where(
                slots == lanes, 1.0, 0.0
            ).astype(BF16)
    copy.wait()
    angles = [column(angle, 1, z.fields)]
    for ref in got:
        code = ref[z.deg * z.per :, :].astype(F32)[:, :1]
        whole = code[: z.fields] * float(CODE) + code[z.fields :]
        angles.append(whole.astype(jnp.int32))
    columns = lax.broadcasted_iota(jnp.int32, (1, z.cols), 1) + base
    cosine, sine = phases(jnp.concatenate(angles, axis=0), columns)
    cos_ref[...] = cosine
    sin_ref[...] = sine
    finish(copies)


def place_kernel(z, order, after, q_ref):
    orders = jnp.concatenate(relative_orders(z, order), axis=1)
    base = lax.axis_index("sub") * z.cols
    step = min(z.cols, LANES)

    @pl.loop(0, z.cols // step)
    def _(b):
        at = pl.multiple_of(b * step, step)
        index = lax.broadcasted_iota(jnp.int32, (step, z.orders), 0) + (base + at)
        q_ref[pl.ds(at, step), :] = jnp.where(index == orders, 1.0, 0.0).astype(BF16)


def fetch_kernel(z, picks, table, *refs):
    outs, sems = refs[: len(picks)], refs[len(picks)]
    finish(fetches(z, table, picks, outs, sems))


def spread(pieces, p_ref, first):
    n_m = p_ref.shape[1]
    block = min(n_m, 1024)
    out = []
    for b in range(n_m // block):
        at, total = first, None
        for piece in pieces:
            width = piece.shape[1]
            part = jnp.dot(
                piece[...], p_ref[at : at + width, b * block : (b + 1) * block], preferred_element_type=F32
            )
            total = part if total is None else total + part
            at += width
        out.append(total)
    return out


def spread_kernel(n, *refs):
    pieces, (p_ref, out) = refs[:n], refs[n:]
    parts = spread(pieces, p_ref, 0)
    block = parts[0].shape[1]
    for b, part in enumerate(parts):
        out[:, b * block : (b + 1) * block] = part.astype(BF16)


def degree_turn(z, k, natural, at, tables, degree, cos_ref, sin_ref, out, to):
    columns = lax.broadcasted_iota(jnp.int32, (1, z.cols), 1) + lax.axis_index("sub") * z.cols
    own = lax.axis_index("deg") * z.held + lax.axis_index("fld") * z.own
    live_c, live_s = live_pair(columns, degree[own + k])
    x = live_c * jnp.dot(natural[at], tables[0][...], preferred_element_type=F32)
    y = live_s * jnp.dot(natural[at + 1], tables[1][...], preferred_element_type=F32)
    cosine, sine = cos_ref[...], sin_ref[...]
    out[to] = (cosine * x - sine * y).astype(BF16)
    out[to + 1] = (sine * x + cosine * y).astype(BF16)


def turn_kernel(z, n, picks, degree, *refs):
    pieces = refs[:n]
    half, p_ref, cos_ref, sin_ref = refs[n : n + 4]
    refs = refs[n + 4 :]
    held = 2 * z.kept
    tables, table, refs = refs[:held], refs[held], refs[held + 1 :]
    out, natural = refs[:2]
    outs, sems = refs[2 : 2 + len(picks)], refs[2 + len(picks)]
    copies = fetches(z, table, picks, outs, sems)
    first = p_ref.shape[0] - sum(piece.shape[1] for piece in pieces)
    parts = spread(pieces, p_ref, first)
    block = parts[0].shape[1]
    for b, part in enumerate(parts):
        part = part + half[:, b * block : (b + 1) * block].astype(F32)
        for r in range(2 * z.own):
            rows = [
                part[j * z.per + r * z.fields : j * z.per + (r + 1) * z.fields] for j in range(z.fld)
            ]
            natural[r, :, b * block : (b + 1) * block] = jnp.concatenate(rows, axis=0).astype(BF16)
    for k in range(z.kept):
        degree_turn(z, k, natural, 2 * k, tables[2 * k : 2 * k + 2], degree, cos_ref, sin_ref, out, 2 * k)
    finish(copies)


def next_turn_kernel(z, chunk, degree, natural, cos_ref, sin_ref, *refs):
    tables, out = refs[:-1], refs[-1]
    for i in range(z.kept):
        k = chunk * z.kept + i
        degree_turn(z, k, natural, 2 * k, tables[2 * i : 2 * i + 2], degree, cos_ref, sin_ref, out, 2 * i)


def part_kernel(z, mid, *refs):
    tables, out = refs[:-1], refs[-1]
    at = pl.multiple_of(lax.axis_index("sub") * z.cols, z.cols)
    for r, table in enumerate(tables):
        out[r] = jnp.dot(mid[r], table[pl.ds(at, z.cols), :], preferred_element_type=F32)


def second_kernel(z, chunk, n, degree, *refs):
    mids = refs[:n]
    part, q_ref = refs[n : n + 2]
    tables = refs[n + 2 : n + 2 + 2 * z.kept]
    outs, held = refs[n + 2 + 2 * z.kept : -1], refs[-1]
    d, s, c = here()
    columns = lax.broadcasted_iota(jnp.int32, (1, z.cols), 1) + s * z.cols
    own = d * z.held + c * z.own + chunk * z.kept
    per = 2 * z.kept * z.fields
    for k in range(z.kept):
        lives = live_pair(columns, degree[own + k])
        both = []
        for p in range(2):
            r = 2 * k + p
            total = part[r]
            for i, mid in enumerate(mids):
                at = pl.multiple_of((s ^ (i + 1)) * z.cols, z.cols)
                total += jnp.dot(mid[r], tables[r][pl.ds(at, z.cols), :], preferred_element_type=F32)
            both.append(lives[p] * total)
        for j in range(z.fld):
            rows = jnp.concatenate([x[j * z.fields : (j + 1) * z.fields] for x in both], axis=0)
            at = j * per + 2 * k * z.fields
            held[at : at + 2 * z.fields, :] = rows.astype(BF16)
    at = 0
    for out in outs:
        width = out.shape[1]
        out[...] = jnp.dot(held[...], q_ref[:, at : at + width], preferred_element_type=F32).astype(BF16)
        at += width


def last_kernel(z, order, angle, *refs):
    owns = refs[: z.deg * z.chunks]
    gots, out = refs[z.deg * z.chunks : -1], refs[-1]
    d, _, c = here()
    cosine, sine = phases(column(angle, 0, z.fields), own_orders(z, order))
    step = 2 * z.fields
    for b in range(z.deg):
        for h in range(z.chunks):
            for j in range(z.fld):
                for k in range(z.kept):
                    if j == 0:
                        both = owns[b * z.chunks + h][k * step : (k + 1) * step, :]
                    else:
                        both = gots[j - 1][b, h, k * step : (k + 1) * step, :]
                    both = both.astype(F32)
                    x, y = both[: z.fields], both[z.fields :]
                    at = (d ^ b) * z.held + (c ^ j) * z.own + h * z.kept + k
                    out[at, 0] = cosine * x - sine * y
                    out[at, 1] = sine * x + cosine * y


def xor_pairs(size, x):
    return [(i, i ^ x) for i in range(size)]


def swap(x, axis, k):
    return lax.ppermute(x, axis, xor_pairs(lax.axis_size(axis), k))


def per_device(coefficients, delta, order_of, degree_of, angle_index):
    z = Sizes(coefficients, delta)
    shape = jax.ShapeDtypeStruct
    d, s, _ = here()
    angles = angle_index.T
    if z.whole_rows:
        order = order_of.reshape(z.orders // LANES, LANES)
        mine = relative = order
    else:
        mine = lax.dynamic_slice_in_dim(order_of, (d * z.sub + s) * z.slots, z.slots).reshape(1, z.slots)
        relative = order_of.reshape(z.deg, z.sub, z.slots)[
            (d ^ jnp.arange(z.deg))[None, :], (s ^ jnp.arange(z.sub))[:, None]
        ].reshape(z.orders // LANES, LANES)

    extra = 2 * z.fields
    firsts = call(
        functools.partial(first_kernel, z),
        [shape((z.deg * z.per + (extra if j else 0), z.slots), BF16) for j in range(z.fld)],
        (coefficients, degree_of, mine, angles),
        [HBM] * 4,
        [VMEM] * z.fld,
        "first",
        moved=4 * coefficients.size,
        scratch=[
            pltpu.VMEM(coefficients.shape, BF16),
            pltpu.SMEM(degree_of.shape, jnp.int32),
            pltpu.VMEM(mine.shape, jnp.int32),
            pltpu.SMEM(angles.shape, jnp.int32),
            pltpu.SemaphoreType.DMA((4,)),
        ],
    )
    firsts = [firsts[0]] + [swap(firsts[j], "fld", j) for j in range(1, z.fld)]

    total = 2 * z.own
    cuts = [0, 3 * total // 8, 5 * total // 8, total]
    groups = [list(range(a, b)) for a, b in zip(cuts, cuts[1:])]
    buffer = pltpu.VMEM((z.orders, z.cols), BF16)
    pieces = 4

    def sems(picks):
        return pltpu.SemaphoreType.DMA((len(picks), pieces))

    moved = 2 * z.orders * z.cols
    p_ref, cos_ref, sin_ref, *tables = call(
        functools.partial(select_kernel, z, groups[0]),
        [
            pltpu.VMEM((z.orders, z.orders), BF16),
            pltpu.VMEM((z.fld * z.fields, z.cols), F32),
            pltpu.VMEM((z.fld * z.fields, z.cols), F32),
        ]
        + [buffer] * len(groups[0]),
        (relative, angles, delta, *firsts[1:]),
        [VMEM, HBM, HBM] + [VMEM] * (z.fld - 1),
        [VMEM] * (3 + len(groups[0])),
        "select",
        moved=moved * len(groups[0]),
        scratch=[
            pltpu.SMEM(angles.shape, jnp.int32),
            pltpu.SemaphoreType.DMA,
            sems(groups[0]),
        ],
    )
    tables += call(
        functools.partial(fetch_kernel, z, groups[1]),
        [buffer] * len(groups[1]),
        (delta,),
        [HBM],
        [VMEM] * len(groups[1]),
        "fetch",
        moved=moved * len(groups[1]),
        scratch=[sems(groups[1])],
    )

    def block(j):
        return jnp.concatenate([x[j * z.per : (j + 1) * z.per] for x in firsts], axis=0)

    arrived = [block(0)] + [swap(block(j), "deg", j) for j in range(1, z.deg)]
    if z.deg * z.sub > 8:
        arrived = [jnp.concatenate(arrived, axis=1)]
    others = [swap(x, "sub", i) for i in range(1, z.sub) for x in arrived]
    n = len(arrived)
    half = call(
        functools.partial(spread_kernel, n),
        pltpu.VMEM((z.rows, z.orders), BF16),
        (*arrived, p_ref),
        [VMEM] * (n + 1),
        VMEM,
        "spread",
        flops=2 * z.rows * z.deg * z.slots * z.orders,
    )
    n = len(others)
    chunk_rows = z.fld * 2 * z.kept * z.fields
    mid_shape = shape((2 * z.kept, z.fld * z.fields, z.cols), BF16)
    mid, natural, *late = call(
        functools.partial(turn_kernel, z, n, groups[2]),
        [mid_shape, pltpu.VMEM((total, z.fld * z.fields, z.orders), BF16)] + [buffer] * len(groups[2]),
        (degree_of, *others, half, p_ref, cos_ref, sin_ref, *tables[: 2 * z.kept], delta),
        [SMEM] + [VMEM] * (n + 4 + 2 * z.kept) + [HBM],
        [VMEM] * (2 + len(groups[2])),
        "turn",
        flops=2 * z.rows * z.orders * (z.orders + z.cols),
        moved=moved * len(groups[2]),
        scratch=[sems(groups[2])],
    )
    tables += late
    q_ref = call(
        functools.partial(place_kernel, z),
        pltpu.VMEM((z.cols, z.orders), BF16),
        (relative, natural),
        [VMEM] * 2,
        VMEM,
        "place",
        moved=2 * z.cols * z.orders,
    )
    mids = [mid]
    for h in range(1, z.chunks):
        used = tables[2 * h * z.kept : 2 * (h + 1) * z.kept]
        mids.append(
            call(
                functools.partial(next_turn_kernel, z, h),
                mid_shape,
                (degree_of, natural, cos_ref, sin_ref, *used),
                [SMEM] + [VMEM] * (3 + len(used)),
                VMEM,
                f"turn{h}",
                flops=2 * chunk_rows * z.orders * z.cols,
            )
        )
    blocks = []
    for h, mid in enumerate(mids):
        used = tables[2 * h * z.kept : 2 * (h + 1) * z.kept]
        others = [swap(mid, "sub", i) for i in range(1, z.sub)]
        part = call(
            functools.partial(part_kernel, z),
            pltpu.VMEM((2 * z.kept, z.fld * z.fields, z.cols), F32),
            (mid, *used),
            [VMEM] * (1 + len(used)),
            VMEM,
            f"part{h}",
            flops=2 * chunk_rows * z.cols * z.cols,
        )
        width = z.deg * z.slots
        outs = call(
            functools.partial(second_kernel, z, h, len(others)),
            [shape((chunk_rows, width), BF16)] * z.sub,
            (degree_of, *others, part, q_ref, *used),
            [SMEM] + [VMEM] * (len(others) + 2 + len(used)),
            [VMEM] * z.sub,
            f"second{h}",
            flops=2 * chunk_rows * z.cols * (2 * z.orders - z.cols),
            scratch=[pltpu.VMEM((chunk_rows, z.cols), BF16)],
        )
        whole = outs[0]
        for i in range(1, z.sub):
            whole = whole + swap(outs[i], "sub", i)
        parts = [whole[:, j * z.slots : (j + 1) * z.slots] for j in range(z.deg)]
        blocks.append([parts[0]] + [swap(parts[j], "deg", j) for j in range(1, z.deg)])
    per = 2 * z.kept * z.fields
    gots = [
        swap(
            jnp.stack([jnp.stack([x[b][j * per : (j + 1) * per] for x in blocks]) for b in range(z.deg)]),
            "fld",
            j,
        )
        for j in range(1, z.fld)
    ]
    owns = [x[b] for b in range(z.deg) for x in blocks]
    return call(
        functools.partial(last_kernel, z),
        shape((z.deg * z.held,) + coefficients.shape[1:], F32),
        (mine, angles, *owns, *gots),
        [VMEM, SMEM] + [VMEM] * (len(owns) + len(gots)),
        VMEM,
        "last",
        moved=6 * coefficients.size,
        vmem=6 * MIB,
    )


def solution(mesh):
    in_specs = (
        P(None, None, ("groups", "fld"), ("deg", "sub")),
        P("deg", None, None, "sub"),
        P(),
        P(),
        P(("groups", "fld"), None),
    )
    out_specs = P(None, None, ("groups", "fld"), ("deg", "sub"))
    return jax.shard_map(per_device, mesh=mesh, in_specs=in_specs, out_specs=out_specs, check_vma=False)
```
